256 devices in a mesh: expert: 64 (over z, x, core), hidden: 4 (over y).
Axes of the slice: x: 4, y: 4, z: 8, core: 2. Of those that a mesh axis runs over, the one named last changes fastest.
Arguments:
- tokens: bfloat16 [8192, 4096], P('expert', 'hidden'), may hold values from -6 to 6
- expert_ids: int32 [8192, 8], P('expert'), may hold values from 0 to 63, all different within a row; in each aligned block of 128 rows (0 to 127, 128 to 255, ...) at most 24 rows name the same one
- combine_weights: float32 [8192, 8], P('expert'), may hold values from 0.2 to 1
- gate_weight: bfloat16 [64, 4096, 1536], P('expert', None, 'hidden'), may hold values from -0.09375 to 0.09375
- up_weight: bfloat16 [64, 4096, 1536], P('expert', None, 'hidden'), may hold values from -0.09375 to 0.09375
- down_weight: bfloat16 [64, 1536, 4096], P('expert', 'hidden'), may hold values from -0.15625 to 0.15625
Outputs:
- mixed: bfloat16 [8192, 4096], P('expert', 'hidden')
The draws below stay inside these ranges and needn't reach their ends.
Inputs may be any that keep to these rules, and one draw needn't show every extreme that they name: `expert_ids`: each row names 8 different experts. Within the rows of one index of expert (aligned blocks of 128 rows) no expert is named by more than 24 rows, a bound that some block reaches.
All inputs are finite; a program needn't handle non-finite values.
Results may differ from the reference program's by a relative error of at most 0.0058.
Values may be sent and summed in bfloat16 or wider, within the bound.
No kernel may reach another device: no remote copies, remote signals or barrier semaphores. Data moves between devices by JAX's collectives and lax.ppermute only.
A program may use at most 128 MiB of HBM per device.

```python
import math
import jax
import jax.numpy as jnp
import numpy as np
from jax import lax

D = 4096
FF = 1536
TOP = 8
EXPERTS = 64
TOK_DEV = 128
TOKENS = 8192
CAP = 24
N_EXPERT = 64
N_HIDDEN = 4


def block_levels(key, extent, pieces, least, high):
    loudness = 1.0
    for axis_at, parts in pieces:
        draws = jax.random.uniform(jax.random.fold_in(jax.random.fold_in(key, 6), axis_at), (parts,), jnp.float32, least / len(pieces), high / len(pieces))
        loudness = loudness * jnp.repeat(jnp.exp(draws), extent[axis_at] // parts).reshape((-1,) + (1,) * (len(extent) - 1 - axis_at))
    return loudness


def deal_out(own_key, own, number, rows, count, top, bound, skew):
    ranking = jax.random.permutation(own_key, count)
    packed, ordinary = shares(count, rows * top, bound, skew, True), shares(count, rows * top, bound, skew, False)
    places = jnp.arange(count)

    def named(tallies, turn):
        used = int((tallies > 0).sum())
        fixed = max(1, used // 4)
        passed = fixed + (places - fixed + turn * (used - fixed)) % max(1, count - fixed)
        return jnp.zeros((count,), jnp.int32).at[ranking[jnp.where(places < fixed, places, passed)]].set(jnp.asarray(tallies, jnp.int32))

    tallies = jnp.where(number % 4 == 0, named(packed, number // 4), named(ordinary, number - number // 4 - 1))
    mixed = jax.random.permutation(jax.random.fold_in(own, 3), count)
    donor, sink = mixed[0:count // 2 * 2:2], mixed[1:count // 2 * 2:2]
    room = jnp.minimum(tallies[donor] - 1, bound - tallies[sink]) // 2
    room = jnp.where((donor == ranking[0]) | (sink == ranking[0]) | (tallies[sink] == 0), 0, jnp.maximum(room, 0))
    passed = jax.random.randint(jax.random.fold_in(own, 4), (count // 2,), 0, 1 << 20) % (room + 1)
    tallies = tallies.at[donor].add(-passed).at[sink].add(passed)
    items = jnp.searchsorted(jnp.cumsum(tallies), jnp.arange(rows * top), side="right").astype(jnp.int32)
    table = items.reshape(top, rows).T
    table = table[jax.random.permutation(jax.random.fold_in(own, 1), rows)]
    turn = jax.random.randint(jax.random.fold_in(own, 2), (rows, 1), 0, top)
    return jnp.take_along_axis(table, (jnp.arange(top)[None, :] + turn) % top, axis=1)


def shares(count, total, reach, slope, full):
    weights = [(1 << 20) // math.isqrt(standing ** slope) + 1 for standing in range(1, count + 1)]
    largest = reach if full else min(reach, max(-(-total // count), total * weights[0] // sum(weights)))
    least = 1 if total - largest >= count - 1 else 0
    given, surplus = [largest] + [least] * (count - 1), total - largest - least * (count - 1)
    while surplus > 0:
        movable = [i for i in range(1, count) if given[i] < largest] or [i for i in range(1, count) if given[i] < reach]
        mass, remaining = sum([weights[i] for i in movable]), surplus
        for i in movable:
            extra = min(reach - given[i], max(1, remaining * weights[i] // mass), surplus)
            given[i] = given[i] + extra
            surplus = surplus - extra
    return np.array(given)


def noise(stream_key, dims, width, limit, shards=(), kind=jnp.bfloat16):
    drawn = jax.random.normal(stream_key, dims, jnp.float32) * width
    if len(shards) > 0:
        drawn = block_levels(stream_key, dims, shards, -0.22, 0.18) * drawn
    return jnp.clip(drawn, min=-limit, max=limit).astype(kind)


def setup_inputs(seed: int = 0) -> dict:
    streams_of = jax.random.split(jax.random.key(seed), 7)
    tokens = noise(streams_of[0], (TOKENS, D), 1.0, 6.0, ((0, 64), (1, 4)))
    expert_ids_keys = jax.random.split(jax.random.fold_in(streams_of[1], 1), TOKENS // TOK_DEV)
    expert_ids_turns = jax.random.permutation(jax.random.fold_in(streams_of[1], 3), TOKENS // TOK_DEV)
    expert_ids = jax.vmap(lambda own, number: deal_out(jax.random.fold_in(streams_of[1], 2), own, number, TOK_DEV, EXPERTS, TOP, CAP, 2))(expert_ids_keys, expert_ids_turns).reshape((TOKENS, TOP))
    combine_weights = jnp.clip(0.2 + 0.8 * jax.random.uniform(streams_of[2], (TOKENS, TOP), jnp.float32) ** block_levels(streams_of[2], (TOKENS, TOP), ((0, 64),), -0.2, 0.2), 0.2, 1.0)
    gate_weight = noise(streams_of[3], (EXPERTS, D, FF), D ** -0.5, 0.09375, ((0, 64), (2, 4)))
    up_weight = noise(streams_of[4], (EXPERTS, D, FF), D ** -0.5, 0.09375, ((0, 64), (2, 4)))
    down_weight = noise(streams_of[5], (EXPERTS, FF, D), FF ** -0.5, 0.15625, ((0, 64), (1, 4)))
    return dict(tokens=tokens, expert_ids=expert_ids, combine_weights=combine_weights, gate_weight=gate_weight, up_weight=up_weight, down_weight=down_weight)


def reference(tokens, expert_ids, combine_weights, gate_weight, up_weight, down_weight):
    block_ids = expert_ids.reshape(N_EXPERT, TOK_DEV * TOP)
    onehot_table = (block_ids[:, :, None] == jnp.arange(EXPERTS, dtype=jnp.int32)[None, None, :]).astype(jnp.int32)
    slot_rank = jnp.sum((jnp.cumsum(onehot_table, axis=1) - 1) * onehot_table, axis=2).astype(jnp.int32)
    source_block = jnp.arange(N_EXPERT, dtype=jnp.int32)[:, None]
    table_pos = ((block_ids * N_EXPERT + source_block) * CAP + slot_rank).astype(jnp.int32)
    token_index = (source_block * TOK_DEV + jnp.arange(TOK_DEV * TOP, dtype=jnp.int32)[None, :] // TOP).astype(jnp.int32)
    total_slots = EXPERTS * N_EXPERT * CAP
    token_table = jnp.full((total_slots,), TOKENS, jnp.int32).at[table_pos.reshape(-1)].set(token_index.reshape(-1))
    weight_table = jnp.zeros((total_slots,), jnp.float32).at[table_pos.reshape(-1)].set(combine_weights.reshape(-1))
    padded = jnp.concatenate([tokens, jnp.zeros((1, D), tokens.dtype)], axis=0)
    quarter = FF // N_HIDDEN

    def one_expert(totals, inputs):
        gate_block, up_block, down_block, row_index, row_weight = inputs
        rows = padded[row_index]
        gate_val = jnp.dot(rows, gate_block, preferred_element_type=jnp.float32)
        up_val = jnp.dot(rows, up_block, preferred_element_type=jnp.float32)
        active = (jax.nn.silu(gate_val) * up_val).astype(jnp.bfloat16)
        out_rows = jnp.zeros((rows.shape[0], D), jnp.float32)
        for block in range(N_HIDDEN):
            partial_value = jnp.dot(active[:, block * quarter:(block + 1) * quarter], down_block[block * quarter:(block + 1) * quarter], preferred_element_type=jnp.float32).astype(jnp.bfloat16)
            out_rows = out_rows + lax.optimization_barrier(partial_value).astype(jnp.float32)
        totals = totals.at[row_index].add(row_weight[:, None] * out_rows)
        return totals, None

    start = jnp.zeros((TOKENS + 1, D), jnp.float32)
    totals, _ = lax.scan(one_expert, start, (gate_weight, up_weight, down_weight, token_table.reshape(EXPERTS, -1), weight_table.reshape(EXPERTS, -1)))
    return totals[:TOKENS].astype(jnp.bfloat16)
```

```python
import jax
import jax.numpy as jnp
from jax import lax
from jax.sharding import PartitionSpec as P


SLOTS = 8


def route(expert_ids, combine_weights, experts):
    ids = expert_ids.T
    weights = combine_weights.T
    rows = ids.shape[1]
    hit = ids[:, None, :] == jnp.arange(experts, dtype=jnp.int32)[None, :, None]
    chosen = jnp.any(hit, axis=0)
    weight = jnp.sum(jnp.where(hit, weights[:, None, :], 0.0), axis=0)
    before = jnp.triu(jnp.ones((rows, rows), jnp.bfloat16), 1)
    rank = jnp.dot(chosen.astype(jnp.bfloat16), before, preferred_element_type=jnp.float32)
    return jnp.where(chosen, rank.astype(jnp.int32), -1), weight


def shift(value, step, size):
    return lax.ppermute(value, "hidden", [(i, (i + step) % size) for i in range(size)])


def ring_gather(shard, size):
    half = shard.shape[0] // 2
    from_left = shift(shard, 1, size)
    from_right = shift(shard, -1, size)
    top = shift(from_left[:half], 1, size)
    bottom = shift(from_right[half:], -1, size)
    return [shard, from_left, from_right, jnp.concatenate([top, bottom], axis=0)]


def on_device(tokens, expert_ids, combine_weights, gate_weight, up_weight, down_weight):
    experts = lax.axis_size("expert")
    size = lax.axis_size("hidden")
    me = lax.axis_index("hidden")
    tok_rows, top_count = expert_ids.shape
    width = tokens.shape[1]
    capacity = min(tok_rows, 3 * tok_rows * top_count // (2 * experts))
    down_block = down_weight[0]
    order = (0, -1, 1, 2)

    def columns(step):
        at = lax.rem(me + step + size, size) * width
        return lax.dynamic_slice(down_block, (0, at), (down_block.shape[0], width))

    down = [columns(0), shift(columns(1), 1, size), shift(columns(-1), -1, size), shift(columns(2), 2, size)]

    def feature_rows(step):
        at = lax.rem(me + step + size, size) * width
        gate_rows = lax.dynamic_slice(gate_weight[0], (at, 0), (width, gate_weight.shape[2]))
        up_rows = lax.dynamic_slice(up_weight[0], (at, 0), (width, up_weight.shape[2]))
        return jnp.concatenate([gate_rows, up_rows], axis=1)

    gate_up = [feature_rows(step) for step in order]
    hidden = gate_weight.shape[2]
    rank, weight = route(expert_ids, combine_weights, experts)
    chunks = capacity // SLOTS

    def picks(chunk):
        slots = jnp.arange(chunk * SLOTS, (chunk + 1) * SLOTS, dtype=jnp.int32)
        return rank[:, None, :] == slots[None, :, None]

    received = []
    for chunk in range(chunks):
        pick = picks(chunk).astype(jnp.bfloat16).reshape(experts * SLOTS, tok_rows)
        send = jnp.dot(pick, tokens, preferred_element_type=jnp.float32).astype(jnp.bfloat16)
        send = send.reshape(experts, SLOTS, width)
        received.append(lax.all_to_all(send, "expert", split_axis=0, concat_axis=0, tiled=True))

    total = jnp.zeros((tok_rows, width), jnp.float32)
    for chunk in range(chunks):
        blocks = ring_gather(received[chunk].reshape(experts * SLOTS, width), size)
        both = sum(
            jnp.dot(block, rows, preferred_element_type=jnp.float32)
            for block, rows in zip(blocks, gate_up)
        )
        active = (jax.nn.silu(both[:, :hidden]) * both[:, hidden:]).astype(jnp.bfloat16)
        actives = ring_gather(active, size)
        out = sum(
            jnp.dot(part, rows, preferred_element_type=jnp.float32)
            for part, rows in zip(actives, down)
        )
        out = out.astype(jnp.bfloat16).reshape(experts, SLOTS, width)
        back = lax.all_to_all(out, "expert", split_axis=0, concat_axis=0, tiled=True)
        back = back.reshape(experts * SLOTS, width)
        mix = jnp.where(picks(chunk), weight[:, None, :], 0.0).reshape(experts * SLOTS, tok_rows)
        high = mix.astype(jnp.bfloat16)
        low = (mix - high.astype(jnp.float32)).astype(jnp.bfloat16)
        for part in (high, low):
            total += lax.dot_general(
                part, back, (((0,), (0,)), ((), ())), preferred_element_type=jnp.float32
            )
    return total.astype(jnp.bfloat16)


def solution(mesh):
    return jax.shard_map(
        on_device,
        mesh=mesh,
        in_specs=(
            P("expert", "hidden"),
            P("expert", None),
            P("expert", None),
            P("expert", None, "hidden"),
            P("expert", None, "hidden"),
            P("expert", "hidden", None),
        ),
        out_specs=P("expert", "hidden"),
        check_vma=False,
    )
```

```python
import functools

import jax
import jax.numpy as jnp
from jax import lax
from jax.experimental import pallas as pl
from jax.experimental.pallas import tpu as pltpu
from jax.sharding import PartitionSpec as P


SLOTS = 8
TILE = 256


def route(expert_ids, combine_weights, experts):
    ids = expert_ids.T
    weights = combine_weights.T
    rows = ids.shape[1]
    hit = ids[:, None, :] == jnp.arange(experts, dtype=jnp.int32)[None, :, None]
    chosen = jnp.any(hit, axis=0)
    weight = jnp.sum(jnp.where(hit, weights[:, None, :], 0.0), axis=0)
    before = jnp.triu(jnp.ones((rows, rows), jnp.bfloat16), 1)
    rank = jnp.dot(chosen.astype(jnp.bfloat16), before, preferred_element_type=jnp.float32)
    return jnp.where(chosen, rank.astype(jnp.int32), -1), weight


def shift(value, step, size):
    return lax.ppermute(value, "hidden", [(i, (i + step) % size) for i in range(size)])


def exchange(value):
    return lax.all_to_all(value, "expert", split_axis=0, concat_axis=0, tiled=True)


def ring_gather(shard, size):
    half = shard.shape[0] // 2
    from_left = shift(shard, 1, size)
    from_right = shift(shard, -1, size)
    top = from_left[:half]
    bottom = from_right[half:]
    top, bottom = shift(top, 1, size), shift(bottom, -1, size)
    return [[shard], [from_left], [from_right], [top, bottom]]


def plain_gather(shard, size, step):
    from_left = shift(shard, 1, size)
    from_right = shift(shard, -1, size)
    far = shift(from_left if step == 1 else from_right, step, size)
    return [[shard], [from_left], [from_right], [far]]


def blocked_dot(row_pieces, weight_copies, start, store, weights, acc, sem):
    waits = []
    for block, (parts, copies) in enumerate(zip(row_pieces, weight_copies)):
        mine, at = list(copies), 0
        for piece, part in enumerate(parts):
            into = store.at[block, pl.ds(at, part.shape[0])]
            mine.append(pltpu.make_async_copy(part, into, sem.at[block, piece]))
            at += part.shape[0]
        waits.append(mine)
    if start is None:
        acc[...] = jnp.zeros_like(acc)
    else:
        waits[0].append(pltpu.make_async_copy(start[0], acc, start[1].at[0]))
    for mine in waits[:2]:
        for copy in mine:
            copy.start()
    tiles = acc.shape[0] // TILE

    def step(index, carry):
        block, tile = index // tiles, index % tiles
        for number, mine in enumerate(waits):

            @pl.when(index == number * tiles)
            def _():
                for copy in mine:
                    copy.wait()
                for copy in waits[number + 2] if number + 2 < len(waits) else ():
                    copy.start()

        rows = pl.ds(pl.multiple_of(tile * TILE, TILE), TILE)
        acc[rows] += jnp.dot(store[block, rows], weights[block], preferred_element_type=jnp.float32)
        return carry

    lax.fori_loop(0, len(waits) * tiles, step, 0)


def take_pieces(refs, counts):
    pieces, at = [], 0
    for count in counts:
        pieces.append(refs[at : at + count])
        at += count
    return pieces, refs[at:]


def gated_kernel(first, given, final, counts, order, *refs):
    pieces, refs = take_pieces(refs, counts)
    start, refs = (refs[0], refs[1:]) if given else (None, refs)
    gate, up, out, store, weights, sem, gate_sem, up_sem, *more = refs
    acc = more.pop(0) if final else out
    width, hidden = weights.shape[1], weights.shape[2] // 2
    copies = []
    for block in range(len(counts)):
        rows = pl.ds(pl.multiple_of(order[first + block] * width, width), width)
        into = weights.at[block]
        copies.append(
            [
                pltpu.make_async_copy(gate.at[0, rows], into.at[:, pl.ds(0, hidden)], gate_sem.at[block]),
                pltpu.make_async_copy(up.at[0, rows], into.at[:, pl.ds(hidden, hidden)], up_sem.at[block]),
            ]
        )
    blocked_dot(pieces, copies, (start, more[0]) if given else None, store, weights, acc, sem)
    if not final:
        return

    def finish(tile, carry):
        rows = pl.ds(pl.multiple_of(tile * TILE, TILE), TILE)
        gate_val = acc[rows, :hidden]
        out[rows] = (gate_val / (1.0 + jnp.exp(-gate_val)) * acc[rows, hidden:]).astype(out.dtype)
        return carry

    lax.fori_loop(0, acc.shape[0] // TILE, finish, 0)


def down_kernel(first, given, counts, order, *refs):
    pieces, refs = take_pieces(refs, counts)
    start, refs = (refs[0], refs[1:]) if given else (None, refs)
    sources, (out, store, weights, sem, weight_sem, *more) = list(refs[: len(counts)]), refs[len(counts) :]
    hidden, width = weights.shape[0] // len(counts), weights.shape[1]
    if first == 0:
        sources[0] = sources[0].at[0, :, pl.ds(pl.multiple_of(order[0] * width, width), width)]
    copies = []
    for block, (parts, source) in enumerate(zip(pieces, sources)):
        place, at = pl.ds(block * hidden, hidden), 0
        copies.append(pltpu.make_async_copy(source, weights.at[place], weight_sem.at[block]))
        for piece, part in enumerate(parts):
            into = store.at[pl.ds(at, part.shape[0]), place]
            copies.append(pltpu.make_async_copy(part, into, sem.at[block, piece]))
            at += part.shape[0]
    if given:
        copies.append(pltpu.make_async_copy(start, more[0], more[1].at[0]))
    for copy in copies:
        copy.start()
    for copy in copies:
        copy.wait()

    def step(tile, carry):
        rows = pl.ds(pl.multiple_of(tile * TILE, TILE), TILE)
        product = jnp.dot(store[rows], weights[...], preferred_element_type=jnp.float32)
        if given:
            product += more[0][rows]
        out[rows] = product.astype(out.dtype)
        return carry

    lax.fori_loop(0, out.shape[0] // TILE, step, 0)


def call_blocked(kernel, order, pieces, others, out, scratch, after, flops, moved):
    counts = tuple(len(parts) for parts in pieces)
    flat = [part for parts in pieces for part in parts]
    spec = pltpu.PrefetchScalarGridSpec(
        num_scalar_prefetch=1,
        grid=(1,),
        in_specs=[pl.BlockSpec(memory_space=pl.ANY)] * (len(flat) + len(others)),
        out_specs=pl.BlockSpec(out.shape, lambda step, order: (0, 0)),
        scratch_shapes=scratch + [pltpu.SemaphoreType.DMA((len(counts), max(counts)))] + after,
    )
    return pl.pallas_call(
        functools.partial(kernel, counts),
        out_shape=out,
        grid_spec=spec,
        cost_estimate=pl.CostEstimate(flops=flops, bytes_accessed=moved, transcendentals=0),
    )(order, *flat, *others)


def gated(order, pieces, gate_weight, up_weight, first=0, start=None, final=True):
    blocks, rows = len(pieces), sum(part.shape[0] for part in pieces[0])
    width, hidden = pieces[0][0].shape[1], gate_weight.shape[2]
    out = (rows, hidden) if final else (rows, 2 * hidden)
    return call_blocked(
        functools.partial(gated_kernel, first, start is not None, final),
        order,
        pieces,
        ([] if start is None else [start]) + [gate_weight, up_weight],
        jax.ShapeDtypeStruct(out, jnp.bfloat16 if final else jnp.float32),
        [
            pltpu.VMEM((blocks, rows, width), jnp.bfloat16),
            pltpu.VMEM((blocks, width, 2 * hidden), jnp.bfloat16),
        ],
        [pltpu.SemaphoreType.DMA((blocks,))] * 2
        + ([pltpu.VMEM((rows, 2 * hidden), jnp.float32)] if final else [])
        + ([] if start is None else [pltpu.SemaphoreType.DMA((1,))]),
        4 * rows * blocks * width * hidden,
        2 * blocks * width * (rows + 2 * hidden),
    )


def projected(order, pieces, down, first=0, start=None, final=True):
    blocks, rows = len(pieces), sum(part.shape[0] for part in pieces[0])
    hidden, width = pieces[0][0].shape[1], down[1].shape[1]
    return call_blocked(
        functools.partial(down_kernel, first, start is not None),
        order,
        pieces,
        ([] if start is None else [start]) + down[first : first + blocks],
        jax.ShapeDtypeStruct((rows, width), jnp.bfloat16 if final else jnp.float32),
        [
            pltpu.VMEM((rows, blocks * hidden), jnp.bfloat16),
            pltpu.VMEM((blocks * hidden, width), jnp.bfloat16),
        ],
        [pltpu.SemaphoreType.DMA((blocks,))]
        + ([] if start is None else [pltpu.VMEM((rows, width), jnp.float32), pltpu.SemaphoreType.DMA((1,))]),
        2 * rows * blocks * width * hidden,
        2 * blocks * hidden * (rows + width) + 2 * rows * width,
    )


A_FORMS = (1, -1, 1)


def joined(parts):
    return parts[0] if len(parts) == 1 else jnp.concatenate(parts, axis=0)


def gated_last(block, rows, early):
    hidden = rows.shape[1] // 2
    late = jnp.dot(block, rows, preferred_element_type=jnp.float32)
    both = early + late
    return (jax.nn.silu(both[:, :hidden]) * both[:, hidden:]).astype(jnp.bfloat16)


def gather(form, shard, size):
    if form == "full":
        return ring_gather(shard, size)
    return plain_gather(shard, size, form)


def on_device(tokens, expert_ids, combine_weights, gate_weight, up_weight, down_weight):
    experts = lax.axis_size("expert")
    size = lax.axis_size("hidden")
    me = lax.axis_index("hidden")
    tok_rows, top_count = expert_ids.shape
    width = tokens.shape[1]
    hidden = gate_weight.shape[2]
    capacity = min(tok_rows, 3 * tok_rows * top_count // (2 * experts))
    order = lax.rem(me + jnp.array([0, size - 1, 1, 2], jnp.int32), size)

    def columns(step):
        at = lax.rem(me + step + size, size) * width
        return lax.dynamic_slice(down_weight[0], (0, at), (hidden, width))

    down = [down_weight, shift(columns(1), 1, size), shift(columns(-1), -1, size), shift(columns(2), 2, size)]
    rank, weight = route(expert_ids, combine_weights, experts)
    rows = experts * SLOTS

    def place(values, first, count):
        slots = jnp.arange(first, first + count, dtype=jnp.int32)
        table = jnp.where(rank[:, None, :] == slots[None, :, None], values, 0.0)
        return table.reshape(experts * count, tok_rows)

    received = []
    for chunk in range(capacity // SLOTS):
        pick = place(1.0, chunk * SLOTS, SLOTS).astype(jnp.bfloat16)
        send = jnp.dot(pick, tokens, preferred_element_type=jnp.float32).astype(jnp.bfloat16)
        received.append(exchange(send.reshape(experts, SLOTS, width)).reshape(rows, width))

    far_at = (lax.rem(me + 2, size) * width, 0)
    far_rows = jnp.concatenate(
        [lax.dynamic_slice(block[0], far_at, (width, hidden)) for block in (gate_weight, up_weight)],
        axis=1,
    )
    outs = []
    for chunk, part in enumerate(received):
        blocks = ring_gather(part, size)
        if chunk + 1 < len(received):
            active = gated(order, blocks, gate_weight, up_weight)
        else:
            early = gated(order, blocks[:3], gate_weight, up_weight, final=False)
            active = gated_last(joined(blocks[3]), far_rows, early)
        blocks = gather(A_FORMS[chunk], active, size)
        if chunk + 1 < len(received):
            out = projected(order, blocks, down)
        else:
            early = projected(order, blocks[:3], down, final=False)
            late = jnp.dot(joined(blocks[3]), down[3], preferred_element_type=jnp.float32)
            out = (early + late).astype(jnp.bfloat16)
        outs.append(out.reshape(experts, SLOTS, width))

    total = jnp.zeros((tok_rows, width), jnp.float32)
    for number, out in enumerate(outs):
        back = exchange(out).reshape(rows, width)
        mix = place(weight[:, None, :], number * SLOTS, SLOTS)
        high = mix.astype(jnp.bfloat16)
        low = (mix - high.astype(jnp.float32)).astype(jnp.bfloat16)
        both = lax.dot_general(
            jnp.concatenate([high, low], axis=1),
            back,
            (((0,), (0,)), ((), ())),
            preferred_element_type=jnp.float32,
        )
        total += both[:tok_rows] + both[tok_rows:]
    return total.astype(jnp.bfloat16)


def solution(mesh):
    return jax.shard_map(
        on_device,
        mesh=mesh,
        in_specs=(
            P("expert", "hidden"),
            P("expert", None),
            P("expert", None),
            P("expert", None, "hidden"),
            P("expert", None, "hidden"),
            P("expert", "hidden", None),
        ),
        out_specs=P("expert", "hidden"),
        check_vma=False,
    )
```
